32 devices in a mesh: groups: 2 (over y), blk: 4 (over x, core), branch: 4 (over z).
Axes of the slice: x: 2, y: 2, z: 4, core: 2. Of those that a mesh axis runs over, the one named last changes fastest.
Arguments:
- queries: bfloat16 [128, 64, 128], P(('groups', 'blk', 'branch')), parts along dimension 0, may hold values from -128 to 128
- new_keys: bfloat16 [128, 8, 128], P(('groups', 'blk', 'branch')), parts along dimension 0, may hold values from -8 to 8
- fresh_token_values: bfloat16 [128, 8, 128], P(('groups', 'blk', 'branch')), parts along dimension 0, may hold values from -6 to 6
- prefix_keys: bfloat16 [16384, 8, 128], P(('groups', 'blk'), 'branch'), parts along dimension 0, may hold values from -4 to 4
- prefix_values: bfloat16 [16384, 8, 128], P(('groups', 'blk'), 'branch'), parts along dimension 0, may hold values from -6 to 6
- suffix_keys: bfloat16 [128, 512, 8, 128], P(('groups', 'blk'), None, 'branch'), parts along dimension 0, may hold values from -8 to 8
- suffix_values: bfloat16 [128, 512, 8, 128], P(('groups', 'blk'), None, 'branch'), parts along dimension 0, may hold values from -6 to 6
- suffix_lengths: int32 [128], P('groups'), parts along dimension 0, may hold values from 1 to 512, 20480 in all
- slot_branch: int32 [128], P('groups'), parts along dimension 0, may hold values from 0 to 63, as said below
Outputs:
- attended: bfloat16 [128, 64, 128], P(('groups', 'blk', 'branch')), parts along dimension 0
The draws below stay inside these ranges and needn't reach their ends.
There are 2 independent parts, one for each index of `groups`. The reference program is written for one: setup_inputs(seed, part) draws one part's arguments, and reference() takes and returns one part's arrays. A program takes and returns all parts, laid end to end along the dimension named above; each array names one. Nothing has to cross between parts.
Inputs may be any that keep to these rules, and one draw needn't show every extreme that they name: slot_branch is a permutation that maps each aligned block of 16 slots onto the branches of the same block of 16 branches.
All inputs are finite; a program needn't handle non-finite values.
Results may differ from the reference program's by a relative error of at most 0.0045.
Values may be sent and summed in bfloat16 or wider, within the bound.
A program may use at most 128 MiB of HBM per device.

```python
import math
import jax
import jax.numpy as jnp
import numpy as np
from jax import lax

H = 64
KVH = 8
HD = 128
SUF = 512
BR_BLK = 16
BRANCHES = 64
PREFIX = 8192


def prefix_base(key):
    raw_keys = jax.random.normal(jax.random.fold_in(key, 11), (PREFIX, KVH, HD), jnp.float32)
    raw_keys = jnp.clip(raw_keys, -4.0, 4.0)
    return raw_keys


def draw_prefix_keys(key, part):
    return prefix_base(key).astype(jnp.bfloat16)


def draw_queries(key, part):
    sample = jnp.clip(jax.random.normal(jax.random.fold_in(key, 12), (BRANCHES, H, HD), jnp.float32) * 3.0, -12.0, 12.0)
    return sample.astype(jnp.bfloat16)


def draw_slot_branch(key, part):
    block_keys = jax.random.split(jax.random.fold_in(key, 21), BRANCHES // BR_BLK)
    orders = jax.vmap(lambda one_key: jax.random.permutation(one_key, BR_BLK))(block_keys)
    offsets = jnp.arange(BRANCHES // BR_BLK, dtype=jnp.int32)[:, None] * BR_BLK
    return (orders.astype(jnp.int32) + offsets).reshape(BRANCHES).astype(jnp.int32)


def block_levels(stream_key, dims, shards, smallest, largest):
    def one(axis_at, blocks):
        draws = jax.random.uniform(jax.random.fold_in(jax.random.fold_in(stream_key, 6), axis_at), (blocks,), jnp.float32, smallest / len(shards), largest / len(shards))
        return jnp.repeat(jnp.exp(draws), dims[axis_at] // blocks).reshape((-1,) + (1,) * (len(dims) - axis_at - 1))

    level = one(*shards[0])
    for cut in shards[1:]:
        level = level * one(*cut)
    return level


def split_up(number_of, total, most, skew):
    weights = [(1 << 20) // math.isqrt(rank ** skew) + 1 for rank in range(2, number_of + 1)]
    spare, holding = total - most - (number_of - 1), [1] * (number_of - 1)
    while spare > 0:
        free = [i for i in range(number_of - 1) if holding[i] < most]
        mass, remaining = sum([weights[i] for i in free]), spare
        for i in free:
            extra = min(most - holding[i], max(1, remaining * weights[i] // mass), spare)
            holding[i] = holding[i] + extra
            spare = spare - extra
    return np.array([most] + holding)


def uneven_parts(own_key, amount, total, bound, lean):
    if amount == 2:
        one = jax.random.randint(own_key, (), max(1, total - bound), min(bound, total - 1) + 1)
        return jnp.stack([one, total - one])
    lengths = jnp.asarray(split_up(amount, total, bound, lean), jnp.int32)
    pairs = (amount - 1) // 2
    source_of, receiver = lengths[1:1 + 2 * pairs:2], lengths[2:2 + 2 * pairs:2]
    margin = jnp.minimum(source_of - 1, bound - receiver)
    passed = jax.random.randint(jax.random.fold_in(own_key, 1), (pairs,), 0, 1 << 20) % (margin + 1)
    lengths = lengths.at[1:1 + 2 * pairs:2].set(source_of - passed).at[2:2 + 2 * pairs:2].set(receiver + passed)
    return lengths[jax.random.permutation(jax.random.fold_in(own_key, 2), amount)]


def scatter_about(key, dims, scale, limit, cuts=(), kind=jnp.bfloat16):
    drawn = scale * jax.random.normal(key, dims, jnp.float32)
    if cuts:
        drawn = drawn * block_levels(key, dims, cuts, -0.22, 0.18)
    return jnp.clip(drawn, -limit, limit).astype(kind)


def setup_inputs(seed: int = 0, part: int = 0) -> dict:
    splits = jax.random.split(jax.random.key(seed), 10)
    part_keys = jax.random.split(jax.random.fold_in(splits[9], part), 10)
    queries = draw_queries(jax.random.fold_in(jax.random.fold_in(splits[9], part), 71), part)
    new_keys = scatter_about(part_keys[1], (BRANCHES, KVH, HD), 1.7, 8.0, ((0, 16),))
    fresh_token_values = scatter_about(part_keys[2], (BRANCHES, KVH, HD), 1.0, 6.0, ((0, 16),))
    prefix_keys = draw_prefix_keys(jax.random.fold_in(jax.random.fold_in(splits[9], part), 71), part)
    prefix_values = scatter_about(part_keys[4], (PREFIX, KVH, HD), 1.0, 6.0, ((0, 4), (1, 4)))
    suffix_keys = scatter_about(part_keys[5], (BRANCHES, SUF, KVH, HD), 1.3, 8.0, ((0, 4), (2, 4)))
    suffix_values = scatter_about(part_keys[6], (BRANCHES, SUF, KVH, HD), 1.0, 6.0, ((0, 4), (2, 4)))
    suffix_lengths = uneven_parts(part_keys[7], BRANCHES, BRANCHES * SUF * 5 // 8, SUF, 2).astype(jnp.int32)
    slot_branch = draw_slot_branch(jax.random.fold_in(jax.random.fold_in(splits[9], part), 71), part)
    return {"queries": queries, "new_keys": new_keys, "fresh_token_values": fresh_token_values, "prefix_keys": prefix_keys, "prefix_values": prefix_values, "suffix_keys": suffix_keys, "suffix_values": suffix_values, "suffix_lengths": suffix_lengths, "slot_branch": slot_branch}


neg_large = -1e+30

def advance(carried, scores, apply_values):
    out_sum, top_score, weight_sum = carried
    new_top = jnp.maximum(top_score, lax.optimization_barrier(jnp.max(scores, axis=-1)))
    rescale = jnp.exp(top_score - new_top)
    weights = jnp.exp(scores - new_top[..., None])
    weight_sum = weight_sum * rescale + lax.optimization_barrier(jnp.sum(weights, axis=-1))
    rounded = lax.optimization_barrier(weights.astype(jnp.bfloat16))
    out_sum = out_sum * rescale[..., None] + apply_values(rounded.astype(jnp.float32))
    return (out_sum, new_top, weight_sum)

def combine(first, second):
    top_score = jnp.maximum(first[1], second[1])
    scale_one = jnp.exp(first[1] - top_score)
    scale_two = jnp.exp(second[1] - top_score)
    out_sum = first[0] * scale_one[..., None] + second[0] * scale_two[..., None]
    weight_sum = first[2] * scale_one + second[2] * scale_two
    return (out_sum, top_score, weight_sum)

def prefix_part(grouped, prefix_keys, prefix_values, score_scale):
    rows, kv_heads, group, head_dim = grouped.shape
    total = prefix_keys.shape[0]
    width = math.gcd(total, 512)
    count = total // width
    query_wide = grouped.astype(jnp.float32)
    key_blocks = prefix_keys.reshape(count, width, kv_heads, head_dim)
    value_blocks = prefix_values.reshape(count, width, kv_heads, head_dim)
    initial = (jnp.zeros((rows, kv_heads, group, head_dim), jnp.float32), jnp.full((rows, kv_heads, group), neg_large, jnp.float32), jnp.zeros((rows, kv_heads, group), jnp.float32))

    def step(carried, blocks):
        key_block, value_block = blocks
        scores = jnp.einsum('rkgd,nkd->rkgn', query_wide, key_block.astype(jnp.float32)) * score_scale

        def apply_values(weights):
            return jnp.einsum('rkgn,nkd->rkgd', weights, value_block.astype(jnp.float32))
        return (advance(carried, scores, apply_values), None)
    final_output, _ = lax.scan(step, initial, (key_blocks, value_blocks))
    return final_output

def suffix_block(arrays, score_scale):
    slot_queries, slot_new_keys, slot_new_values, branch_slot_keys, slot_values, slot_lengths = arrays
    query_wide = slot_queries.astype(jnp.float32)
    group = slot_queries.shape[2]
    own_score = jnp.einsum('skgd,skd->skg', query_wide, slot_new_keys.astype(jnp.float32)) * score_scale
    own_value = jnp.broadcast_to(slot_new_values.astype(jnp.float32)[:, :, None, :], slot_queries.shape)
    carried = (own_value, own_score, jnp.ones_like(own_score))
    scores = jnp.einsum('skgd,snkd->skgn', query_wide, branch_slot_keys.astype(jnp.float32)) * score_scale
    positions = jnp.arange(branch_slot_keys.shape[1], dtype=jnp.int32)
    valid_mask = positions[None, :] < slot_lengths[:, None]
    scores = jnp.where(valid_mask[:, None, None, :], scores, neg_large)
    values_wide = slot_values.astype(jnp.float32)

    def apply_values(weights):
        return jnp.einsum('skgn,snkd->skgd', weights, values_wide)
    return advance(carried, scores, apply_values)

def reference(queries, new_keys, fresh_token_values, prefix_keys, prefix_values, suffix_keys, suffix_values, suffix_lengths, slot_branch):
    group = H // KVH
    score_scale = 1.0 / math.sqrt(HD)
    grouped = queries.reshape(BRANCHES, KVH, group, HD)
    prefix_state = prefix_part(grouped, prefix_keys, prefix_values, score_scale)
    slot_arrays = (grouped[slot_branch], new_keys[slot_branch], fresh_token_values[slot_branch], suffix_keys, suffix_values, suffix_lengths[slot_branch])
    width = math.gcd(BRANCHES, 64)
    count = BRANCHES // width
    stacked = tuple((item.reshape((count, width) + item.shape[1:]) for item in slot_arrays))
    slot_state = lax.map(lambda arrays: suffix_block(arrays, score_scale), stacked)
    slot_state = tuple((member.reshape((BRANCHES,) + member.shape[2:]) for member in slot_state))
    slot_of = jnp.zeros((BRANCHES,), jnp.int32).at[slot_branch].set(jnp.arange(BRANCHES, dtype=jnp.int32))
    suffix_state = tuple((member[slot_of] for member in slot_state))
    out_sum, top_score, weight_sum = combine(prefix_state, suffix_state)
    final_output = (out_sum / weight_sum[..., None]).astype(jnp.bfloat16)
    return final_output.reshape(BRANCHES, H, HD)
```

```python
import functools
import math

import jax
import jax.numpy as jnp
from jax import lax
from jax.experimental import pallas as pl
from jax.experimental.pallas import tpu as pltpu
from jax.sharding import PartitionSpec as P

MESH = pl.DeviceIdType.MESH
F32 = jnp.float32
BF16 = jnp.bfloat16
STAT_ROWS = 16


def kernel(
    cfg,
    q_hbm,
    nk_hbm,
    nv_hbm,
    pk_hbm,
    pv_hbm,
    sk_hbm,
    sv_hbm,
    len_hbm,
    slot_hbm,
    out_ref,
    q_own,
    nk,
    nv,
    pk_raw,
    pv_raw,
    pk_wide,
    pv_wide,
    pk,
    pv,
    sk,
    sv,
    lens,
    slots,
    q_all,
    part_o,
    part_m,
    part_l,
    own_w,
    own_v,
    send_buf,
    recv_buf,
    local_sem,
    send_q,
    recv_q,
    send_p,
    recv_p,
):
    nblk, nbr, rdev, kvl, group, hd, keys, suf = cfg
    n = nblk * nbr
    rows = rdev * nbr
    mrow = rdev * group
    factor = math.log2(math.e) / math.sqrt(hd)
    grp = lax.axis_index("groups")
    my_blk = lax.axis_index("blk")
    my_br = lax.axis_index("branch")
    me = my_blk * nbr + my_br

    def device(p):
        return (grp, lax.div(p, nbr), lax.rem(p, nbr))

    pairs = [
        (q_hbm, q_own),
        (nk_hbm, nk),
        (nv_hbm, nv),
        (pk_hbm, pk_raw),
        (pv_hbm, pv_raw),
        (len_hbm, lens),
        (slot_hbm, slots),
        (sk_hbm, sk),
        (sv_hbm, sv),
    ]
    local = [pltpu.make_async_copy(a, b, local_sem.at[i]) for i, (a, b) in enumerate(pairs)]
    own_q = pltpu.make_async_copy(
        q_hbm.at[:, my_br], q_all.at[pl.ds(me * rdev, rdev)], local_sem.at[len(pairs)]
    )

    barrier = pltpu.get_barrier_semaphore()

    def greet(k, c):
        pl.semaphore_signal(
            barrier, inc=1, device_id=device(lax.rem(me + k, n)), device_id_type=MESH
        )
        return c

    lax.fori_loop(1, n, greet, 0)
    for copy in local[:5]:
        copy.start()
    own_q.start()
    for copy in local[5:]:
        copy.start()
    pl.semaphore_wait(barrier, n - 1)

    def q_copy(p, source):
        return pltpu.make_async_remote_copy(
            src_ref=q_hbm.at[:, lax.rem(p, nbr)],
            dst_ref=q_all.at[pl.ds(source * rdev, rdev)],
            send_sem=send_q.at[p],
            recv_sem=recv_q.at[source],
            device_id=device(p),
            device_id_type=MESH,
        )

    def send_one(k, c):
        q_copy(lax.rem(me + k, n), me).start()
        return c

    lax.fori_loop(1, n, send_one, 0)

    def p_copy(p, source):
        return pltpu.make_async_remote_copy(
            src_ref=send_buf.at[p],
            dst_ref=recv_buf.at[source],
            send_sem=send_p.at[p],
            recv_sem=recv_p.at[source],
            device_id=device(p),
            device_id_type=MESH,
        )

    local[3].wait()
    local[4].wait()
    chunk = math.gcd(keys, 256)

    def spread(t, c):
        at = pl.ds(pl.multiple_of(t * chunk * kvl, chunk * kvl), chunk * kvl)
        for raw, wide, dest in ((pk_raw, pk_wide, pk), (pv_raw, pv_wide, pv)):
            wide[at, :] = raw[at, :].astype(F32)
            for h in range(kvl):
                piece = wide[pl.ds(t * chunk * kvl + h, chunk, stride=kvl), :]
                dest[h, pl.ds(pl.multiple_of(t * chunk, chunk), chunk), :] = piece.astype(BF16)
        return c

    lax.fori_loop(0, keys // chunk, spread, 0)

    for copy in local[:3]:
        copy.wait()
    nk_wide = nk[...].astype(F32)
    nv_wide = nv[...].astype(F32)
    for jj in range(nbr):
        q_wide = q_own[:, jj].astype(F32)
        for h in range(kvl):
            head = jj * kvl + h
            key = nk_wide[:, head : head + 1, :]
            value = nv_wide[:, head : head + 1, :]
            part = q_wide[:, h * group : (h + 1) * group, :]
            score = jnp.sum(part * key, axis=-1, keepdims=True)
            own_w[jj, h] = jnp.broadcast_to(score, (rdev, group, hd)).reshape(mrow, hd)
            own_v[jj, h] = jnp.broadcast_to(value, (rdev, group, hd)).reshape(mrow, hd)

    lane = lax.broadcasted_iota(jnp.int32, (mrow, hd), 1)
    line = lax.broadcasted_iota(jnp.int32, (mrow, hd), 0)
    picks = [lane == line + h * mrow for h in range(kvl)]
    stat_line = lax.broadcasted_iota(jnp.int32, (STAT_ROWS, hd), 0)

    def to_row(columns):
        total = None
        for h in range(kvl):
            one = jnp.sum(jnp.where(picks[h], columns[h], 0.0), axis=0, keepdims=True)
            total = one if total is None else total + one
        return total

    def split(x):
        high = x.astype(BF16).astype(F32)
        rest = x - high
        mid = rest.astype(BF16).astype(F32)
        return [high, mid, rest - mid]

    def build(p, outs, tops, sums):
        for h in range(kvl):
            send_buf[p, h * mrow : (h + 1) * mrow, :] = outs[h].astype(BF16)
        stats = jnp.zeros((STAT_ROWS, hd), F32)
        for i, piece in enumerate(split(to_row(tops)) + split(to_row(sums))):
            stats = jnp.where(stat_line == i, piece, stats)
        send_buf[p, kvl * mrow : kvl * mrow + STAT_ROWS, :] = stats.astype(BF16)

    half = nblk // 2
    my_chip = lax.div(my_blk, 2)
    my_core = lax.rem(my_blk, 2)

    def prefix_step(d, c):
        chip = lax.rem(my_chip + lax.div(d, 2), half)
        core = lax.rem(my_core + lax.rem(d, 2), 2)
        ib = chip * 2 + core

        @pl.when(d < nblk)
        def _():
            for jj in range(nbr):
                q_copy(me, ib * nbr + jj).wait_recv()

        @pl.when(d == nblk)
        def _():
            own_q.wait()
            for k in range(1, nbr):
                q_copy(me, my_blk * nbr + lax.rem(my_br + k, nbr)).wait_recv()

        q_wide = q_all[pl.ds(ib * rows, rows)].astype(F32)
        for h in range(kvl):
            query = q_wide[:, h * group : (h + 1) * group, :].reshape(rows * group, hd)
            scores = lax.dot_general(
                query.astype(BF16), pk[h], (((1,), (1,)), ((), ())), preferred_element_type=F32
            )
            top = jnp.max(scores, axis=1, keepdims=True)
            weights = jnp.exp2((scores - top) * factor)
            total = jnp.sum(weights, axis=1, keepdims=True)
            part_o[h] = jnp.dot(weights.astype(BF16), pv[h], preferred_element_type=F32)
            part_m[h] = jnp.broadcast_to(top, (rows * group, hd))
            part_l[h] = jnp.broadcast_to(total, (rows * group, hd))

        @pl.when(d < nblk)
        def _():
            for jj in range(nbr):
                at = slice(jj * mrow, (jj + 1) * mrow)
                p = ib * nbr + jj
                build(
                    p,
                    [part_o[h, at, :] for h in range(kvl)],
                    [part_m[h, at, :] for h in range(kvl)],
                    [part_l[h, at, :] for h in range(kvl)],
                )
                p_copy(p, me).start()

        return c

    lax.fori_loop(1, nblk + 1, prefix_step, 0)

    for copy in local[5:]:
        copy.wait()
    first = my_blk * rows
    qrow = kvl * group
    wide = suf * kvl
    col = lax.broadcasted_iota(jnp.int32, (qrow, wide), 1)
    row_head = lax.div(lax.broadcasted_iota(jnp.int32, (qrow, wide), 0), group)
    right_head = lax.rem(col, kvl) == row_head
    position = lax.div(col, kvl)

    def suffix_step(k, c):
        jj = lax.rem(my_br + k, nbr)
        keep = []
        for r in range(rdev):
            b = jj * rdev + r
            slot = jnp.int32(0)
            for s in range(rows):
                slot = jnp.where(slots[first + s] == first + b, s, slot)
            scores = lax.dot_general(
                q_all[first + b], sk[slot], (((1,), (1,)), ((), ())), preferred_element_type=F32
            )
            valid = right_head & (position < lens[first + b])
            keep.append((jnp.where(valid, scores, -1e30), slot))
        done = []
        for scores, slot in keep:
            top = jnp.max(scores, axis=1, keepdims=True)
            weights = jnp.exp2((scores - top) * factor)
            total = jnp.sum(weights, axis=1, keepdims=True)
            out = jnp.dot(weights.astype(BF16), sv[slot], preferred_element_type=F32)
            done.append((out, jnp.broadcast_to(top, out.shape), jnp.broadcast_to(total, out.shape)))
        outs, tops, sums = [], [], []
        at = pl.ds(pl.multiple_of(jj * mrow, mrow), mrow)
        for h in range(kvl):
            cut = slice(h * group, (h + 1) * group)
            o2, m2, l2 = (
                jnp.concatenate([item[i][cut] for item in done], axis=0) for i in range(3)
            )
            o1, m1, l1 = part_o[h, at, :], part_m[h, at, :], part_l[h, at, :]
            top = jnp.maximum(m1, m2)
            one = jnp.exp2((m1 - top) * factor)
            two = jnp.exp2((m2 - top) * factor)
            outs.append(o1 * one + o2 * two)
            tops.append(top)
            sums.append(l1 * one + l2 * two)
        p = my_blk * nbr + jj
        build(p, outs, tops, sums)

        @pl.when(k < nbr)
        def _():
            p_copy(p, me).start()

        return c

    lax.fori_loop(1, nbr + 1, suffix_step, 0)
    recv_buf[me] = send_buf[me]

    def wait_one(k, c):
        p_copy(me, lax.rem(me + k, n)).wait_recv()
        return c

    lax.fori_loop(1, n, wait_one, 0)

    def merge(jj, c):
        finals = []
        stats = []
        for ii in range(nblk):
            block = recv_buf[ii * nbr + jj, kvl * mrow : kvl * mrow + STAT_ROWS, :].astype(F32)
            stats.append(
                (block[0:1] + block[1:2] + block[2:3], block[3:4] + block[4:5] + block[5:6])
            )
        for h in range(kvl):
            tops = [
                jnp.sum(jnp.where(picks[h], s[0], 0.0), axis=1, keepdims=True) for s in stats
            ]
            sums = [
                jnp.sum(jnp.where(picks[h], s[1], 0.0), axis=1, keepdims=True) for s in stats
            ]
            mine = own_w[jj, h]
            top = mine
            for t in tops:
                top = jnp.maximum(top, t)
            scale = jnp.exp2((mine - top) * factor)
            num = own_v[jj, h] * scale
            den = scale
            for ii in range(nblk):
                scale = jnp.exp2((tops[ii] - top) * factor)
                piece = recv_buf[ii * nbr + jj, h * mrow : (h + 1) * mrow, :].astype(F32)
                num = num + piece * scale
                den = den + sums[ii] * scale
            finals.append((num / den).reshape(rdev, group, hd))
        out_ref[:, jj] = jnp.concatenate(finals, axis=1).astype(BF16)
        return c

    lax.fori_loop(0, nbr, merge, 0)

    def drain(k, c):
        p = lax.rem(me + k, n)
        q_copy(p, me).wait_send()
        p_copy(p, me).wait_send()
        return c

    lax.fori_loop(1, n, drain, 0)


def solution(mesh):
    nblk, nbr = mesh.shape["blk"], mesh.shape["branch"]

    def per_device(q, nk, nv, pk, pv, sk, sv, lens, slots):
        rdev, heads, hd = q.shape
        keys, kvl = pk.shape[:2]
        nslot, suf = sk.shape[:2]
        hl = heads // nbr
        group = hl // kvl
        n = nblk * nbr
        rows = rdev * nbr
        mrow = rdev * group
        cfg = (nblk, nbr, rdev, kvl, group, hd, keys, suf)
        dma = pltpu.SemaphoreType.DMA
        out = pl.pallas_call(
            functools.partial(kernel, cfg),
            out_shape=jax.ShapeDtypeStruct((rdev, nbr, hl, hd), BF16),
            in_specs=[pl.BlockSpec(memory_space=pl.ANY)] * 9,
            out_specs=pl.BlockSpec(memory_space=pltpu.VMEM),
            scratch_shapes=[
                pltpu.VMEM((rdev, nbr, hl, hd), BF16),
                pltpu.VMEM(nk.shape, BF16),
                pltpu.VMEM(nv.shape, BF16),
                pltpu.VMEM((keys * kvl, hd), BF16),
                pltpu.VMEM((keys * kvl, hd), BF16),
                pltpu.VMEM((keys * kvl, hd), F32),
                pltpu.VMEM((keys * kvl, hd), F32),
                pltpu.VMEM((kvl, keys, hd), BF16),
                pltpu.VMEM((kvl, keys, hd), BF16),
                pltpu.VMEM((nslot, suf * kvl, hd), BF16),
                pltpu.VMEM((nslot, suf * kvl, hd), BF16),
                pltpu.SMEM(lens.shape, jnp.int32),
                pltpu.SMEM(slots.shape, jnp.int32),
                pltpu.VMEM((n * rdev, hl, hd), BF16),
                pltpu.VMEM((kvl, rows * group, hd), F32),
                pltpu.VMEM((kvl, rows * group, hd), F32),
                pltpu.VMEM((kvl, rows * group, hd), F32),
                pltpu.VMEM((nbr, kvl, mrow, hd), F32),
                pltpu.VMEM((nbr, kvl, mrow, hd), F32),
                pltpu.VMEM((n, kvl * mrow + STAT_ROWS, hd), BF16),
                pltpu.VMEM((n, kvl * mrow + STAT_ROWS, hd), BF16),
                dma((10,)),
                dma((n,)),
                dma((n,)),
                dma((n,)),
                dma((n,)),
            ],
            compiler_params=pltpu.CompilerParams(
                collective_id=0, has_side_effects=True, vmem_limit_bytes=60 * 1024 * 1024
            ),
            name="attend",
        )(
            q.reshape(rdev, nbr, hl, hd),
            nk,
            nv,
            pk.reshape(keys * kvl, hd),
            pv.reshape(keys * kvl, hd),
            sk.reshape(nslot, suf * kvl, hd),
            sv.reshape(nslot, suf * kvl, hd),
            lens,
            slots,
        )
        return out.reshape(rdev, heads, hd)

    return jax.shard_map(
        per_device,
        mesh=mesh,
        in_specs=(
            P(("groups", "blk", "branch"), None, None),
            P(("groups", "blk", "branch"), None, None),
            P(("groups", "blk", "branch"), None, None),
            P(("groups", "blk"), "branch", None),
            P(("groups", "blk"), "branch", None),
            P(("groups", "blk"), None, "branch", None),
            P(("groups", "blk"), None, "branch", None),
            P("groups"),
            P("groups"),
        ),
        out_specs=P(("groups", "blk", "branch"), None, None),
        check_vma=False,
    )
```

```python
import functools
import math

import jax
import jax.numpy as jnp
from jax import lax
from jax.experimental import pallas as pl
from jax.experimental.pallas import tpu as pltpu
from jax.sharding import PartitionSpec as P

MESH = pl.DeviceIdType.MESH
F32 = jnp.float32
BF16 = jnp.bfloat16
STAT_ROWS = 16


def kernel(
    cfg,
    q_hbm,
    nk_hbm,
    nv_hbm,
    pk_hbm,
    pv_hbm,
    sk_hbm,
    sv_hbm,
    len_hbm,
    slot_hbm,
    out_ref,
    q_own,
    nk,
    nv,
    pk_raw,
    pv_raw,
    pk_wide,
    pv_wide,
    pk,
    pv,
    sk,
    sv,
    lens,
    slots,
    q_all,
    part_o,
    part_m,
    part_l,
    away_o,
    away_m,
    away_l,
    own_w,
    own_v,
    send_buf,
    recv_buf,
    last_send,
    last_recv,
    local_sem,
    send_q,
    recv_q,
    pass_send,
    pass_recv,
    send_p,
    recv_p,
    send_f,
    recv_f,
):
    nblk, nbr, rdev, kvl, group, hd, keys, suf = cfg
    n = nblk * nbr
    rows = rdev * nbr
    mrow = rdev * group
    factor = math.log2(math.e) / math.sqrt(hd)
    grp = lax.axis_index("groups")
    my_blk = lax.axis_index("blk")
    my_br = lax.axis_index("branch")
    me = my_blk * nbr + my_br

    pairs = [
        (q_hbm, q_own),
        (nk_hbm, nk),
        (nv_hbm, nv),
        (pk_hbm, pk_raw),
        (pv_hbm, pv_raw),
        (len_hbm, lens),
        (slot_hbm, slots),
        (sk_hbm, sk),
        (sv_hbm, sv),
    ]
    local = [pltpu.make_async_copy(a, b, local_sem.at[i]) for i, (a, b) in enumerate(pairs)]
    own_q = pltpu.make_async_copy(
        q_hbm.at[:, my_br], q_all.at[pl.ds(me * rdev, rdev)], local_sem.at[len(pairs)]
    )

    barrier = pltpu.get_barrier_semaphore()

    half = nblk // 2
    my_chip = lax.div(my_blk, 2)
    my_core = lax.rem(my_blk, 2)

    def near(d):
        chip = lax.rem(my_chip + lax.div(d, 2), half)
        return chip * 2 + lax.rem(my_core + lax.rem(d, 2), 2)

    def along(k):
        return lax.rem(my_br + k, nbr)

    def ordered(t):
        return jnp.where(t == nblk - 1, 1, t + 1)

    def greet_branch(k, c):
        pl.semaphore_signal(
            barrier, inc=1, device_id=(grp, my_blk, along(k)), device_id_type=MESH
        )
        return c

    def greet_blk(d, c):
        pl.semaphore_signal(barrier, inc=1, device_id=(grp, near(d), my_br), device_id_type=MESH)
        return c

    lax.fori_loop(1, nbr, greet_branch, 0)
    lax.fori_loop(1, nblk, greet_blk, 0)
    for copy in local[:5]:
        copy.start()
    own_q.start()
    for copy in local[5:]:
        copy.start()
    pl.semaphore_wait(barrier, nbr + nblk - 2)

    def q_copy(j, source):
        return pltpu.make_async_remote_copy(
            src_ref=q_hbm.at[:, j],
            dst_ref=q_all.at[pl.ds((my_blk * nbr + source) * rdev, rdev)],
            send_sem=send_q.at[j],
            recv_sem=recv_q.at[source],
            device_id=(grp, my_blk, j),
            device_id_type=MESH,
        )

    def pass_copy(ib, j, owner, src=None):
        at = pl.ds((owner * nbr + j) * rdev, rdev)
        return pltpu.make_async_remote_copy(
            src_ref=q_all.at[at] if src is None else src,
            dst_ref=q_all.at[at],
            send_sem=pass_send.at[ib * nbr + j],
            recv_sem=pass_recv.at[owner * nbr + j],
            device_id=(grp, ib, my_br),
            device_id_type=MESH,
        )

    def send_one(k, c):
        q_copy(along(k), my_br).start()
        return c

    lax.fori_loop(1, nbr, send_one, 0)

    def pass_own(t, c):
        pass_copy(near(ordered(t)), my_br, my_blk, q_hbm.at[:, my_br]).start()
        return c

    lax.fori_loop(1, nblk, pass_own, 0)

    def p_copy(ib, owner):
        return pltpu.make_async_remote_copy(
            src_ref=send_buf.at[pl.ds(ib * nbr, nbr)],
            dst_ref=recv_buf.at[pl.ds(owner * nbr, nbr)],
            send_sem=send_p.at[ib],
            recv_sem=recv_p.at[owner],
            device_id=(grp, ib, my_br),
            device_id_type=MESH,
        )

    def f_copy(j, source):
        return pltpu.make_async_remote_copy(
            src_ref=last_send.at[j],
            dst_ref=last_recv.at[source],
            send_sem=send_f.at[j],
            recv_sem=recv_f.at[source],
            device_id=(grp, my_blk, j),
            device_id_type=MESH,
        )

    local[3].wait()
    local[4].wait()
    chunk = math.gcd(keys, 256)

    def spread(t, c):
        at = pl.ds(pl.multiple_of(t * chunk * kvl, chunk * kvl), chunk * kvl)
        for raw, wide, dest in ((pk_raw, pk_wide, pk), (pv_raw, pv_wide, pv)):
            wide[at, :] = raw[at, :].astype(F32)
            for h in range(kvl):
                piece = wide[pl.ds(t * chunk * kvl + h, chunk, stride=kvl), :]
                dest[h, pl.ds(pl.multiple_of(t * chunk, chunk), chunk), :] = piece.astype(BF16)
        return c

    lax.fori_loop(0, keys // chunk, spread, 0)

    for copy in local[:3]:
        copy.wait()
    nk_wide = nk[...].astype(F32)
    nv_wide = nv[...].astype(F32)
    for jj in range(nbr):
        q_wide = q_own[:, jj].astype(F32)
        for h in range(kvl):
            head = jj * kvl + h
            key = nk_wide[:, head : head + 1, :]
            value = nv_wide[:, head : head + 1, :]
            part = q_wide[:, h * group : (h + 1) * group, :]
            score = jnp.sum(part * key, axis=-1, keepdims=True)
            own_w[jj, h] = jnp.broadcast_to(score, (rdev, group, hd)).reshape(mrow, hd)
            own_v[jj, h] = jnp.broadcast_to(value, (rdev, group, hd)).reshape(mrow, hd)

    lane = lax.broadcasted_iota(jnp.int32, (mrow, hd), 1)
    line = lax.broadcasted_iota(jnp.int32, (mrow, hd), 0)
    picks = [lane == line + h * mrow for h in range(kvl)]
    stat_line = lax.broadcasted_iota(jnp.int32, (STAT_ROWS, hd), 0)

    def to_row(columns):
        total = None
        for h in range(kvl):
            one = jnp.sum(jnp.where(picks[h], columns[h], 0.0), axis=0, keepdims=True)
            total = one if total is None else total + one
        return total

    def split(x):
        high = x.astype(BF16).astype(F32)
        rest = x - high
        mid = rest.astype(BF16).astype(F32)
        return [high, mid, rest - mid]

    def build(buf, p, outs, tops, sums):
        for h in range(kvl):
            buf[p, h * mrow : (h + 1) * mrow, :] = outs[h].astype(BF16)
        stats = jnp.zeros((STAT_ROWS, hd), F32)
        for i, piece in enumerate(split(to_row(tops)) + split(to_row(sums))):
            stats = jnp.where(stat_line == i, piece, stats)
        buf[p, kvl * mrow : kvl * mrow + STAT_ROWS, :] = stats.astype(BF16)

    def attend(ib, keep_o, keep_m, keep_l):
        q_wide = q_all[pl.ds(ib * rows, rows)].astype(F32)
        for h in range(kvl):
            query = q_wide[:, h * group : (h + 1) * group, :].reshape(rows * group, hd)
            scores = lax.dot_general(
                query.astype(BF16), pk[h], (((1,), (1,)), ((), ())), preferred_element_type=F32
            )
            top = jnp.max(scores, axis=1, keepdims=True)
            weights = jnp.exp2((scores - top) * factor)
            total = jnp.sum(weights, axis=1, keepdims=True)
            keep_o[h] = jnp.dot(weights.astype(BF16), pv[h], preferred_element_type=F32)
            keep_m[h] = jnp.broadcast_to(top, (rows * group, hd))
            keep_l[h] = jnp.broadcast_to(total, (rows * group, hd))

    def relay(k, c):
        j = along(k)
        q_copy(my_br, j).wait_recv()

        def forward(t, c):
            pass_copy(near(ordered(t)), j, my_blk).start()
            return c

        return lax.fori_loop(1, nblk, forward, c)

    lax.fori_loop(1, nbr, relay, 0)
    own_q.wait()
    attend(my_blk, part_o, part_m, part_l)

    for copy in local[5:]:
        copy.wait()
    first = my_blk * rows
    qrow = kvl * group
    wide = suf * kvl
    col = lax.broadcasted_iota(jnp.int32, (qrow, wide), 1)
    row_head = lax.div(lax.broadcasted_iota(jnp.int32, (qrow, wide), 0), group)
    right_head = lax.rem(col, kvl) == row_head
    position = lax.div(col, kvl)

    def suffix_step(jj, c):
        keep = []
        for r in range(rdev):
            b = jj * rdev + r
            slot = jnp.int32(0)
            for s in range(rows):
                slot = jnp.where(slots[first + s] == first + b, s, slot)
            scores = lax.dot_general(
                q_all[first + b], sk[slot], (((1,), (1,)), ((), ())), preferred_element_type=F32
            )
            valid = right_head & (position < lens[first + b])
            keep.append((jnp.where(valid, scores, -1e30), slot))
        done = []
        for scores, slot in keep:
            top = jnp.max(scores, axis=1, keepdims=True)
            weights = jnp.exp2((scores - top) * factor)
            total = jnp.sum(weights, axis=1, keepdims=True)
            out = jnp.dot(weights.astype(BF16), sv[slot], preferred_element_type=F32)
            done.append((out, jnp.broadcast_to(top, out.shape), jnp.broadcast_to(total, out.shape)))
        at = pl.ds(pl.multiple_of(jj * mrow, mrow), mrow)
        for h in range(kvl):
            cut = slice(h * group, (h + 1) * group)
            o2, m2, l2 = (
                jnp.concatenate([item[i][cut] for item in done], axis=0) for i in range(3)
            )
            o1, m1, l1 = part_o[h, at, :], part_m[h, at, :], part_l[h, at, :]
            top = jnp.maximum(m1, m2)
            one = jnp.exp2((m1 - top) * factor)
            two = jnp.exp2((m2 - top) * factor)
            part_o[h, at, :] = o1 * one + o2 * two
            part_m[h, at, :] = top
            part_l[h, at, :] = l1 * one + l2 * two
        return c

    lax.fori_loop(0, nbr, suffix_step, 0)

    def prefix_step(t, c):
        ib = near(ordered(t))

        def arrive(j, c):
            pass_copy(my_blk, j, ib).wait_recv()
            return c

        lax.fori_loop(0, nbr, arrive, 0)
        attend(ib, away_o, away_m, away_l)
        for jj in range(nbr):
            at = slice(jj * mrow, (jj + 1) * mrow)
            build(
                send_buf,
                ib * nbr + jj,
                [away_o[h, at, :] for h in range(kvl)],
                [away_m[h, at, :] for h in range(kvl)],
                [away_l[h, at, :] for h in range(kvl)],
            )
        p_copy(ib, my_blk).start()
        return c

    lax.fori_loop(1, nblk, prefix_step, 0)

    def wait_one(d, c):
        p_copy(my_blk, near(d)).wait_recv()
        return c

    lax.fori_loop(1, nblk, wait_one, 0)

    def read_stats(buf, p):
        block = buf[p, kvl * mrow : kvl * mrow + STAT_ROWS, :].astype(F32)
        return (block[0:1] + block[1:2] + block[2:3], block[3:4] + block[4:5] + block[5:6])

    def to_column(h, row):
        return jnp.sum(jnp.where(picks[h], row, 0.0), axis=1, keepdims=True)

    def gather(k, c):
        jj = along(k)
        at = pl.ds(pl.multiple_of(jj * mrow, mrow), mrow)
        sources = [near(d) * nbr + jj for d in range(1, nblk)]
        stats = [read_stats(recv_buf, p) for p in sources]
        outs, tops, sums = [], [], []
        for h in range(kvl):
            heights = [to_column(h, item[0]) for item in stats]
            mine = part_m[h, at, :]
            top = mine
            for height in heights:
                top = jnp.maximum(top, height)
            scale = jnp.exp2((mine - top) * factor)
            num = part_o[h, at, :] * scale
            den = part_l[h, at, :] * scale
            for p, item, height in zip(sources, stats, heights):
                scale = jnp.exp2((height - top) * factor)
                num = num + recv_buf[p, h * mrow : (h + 1) * mrow, :].astype(F32) * scale
                den = den + to_column(h, item[1]) * scale
            outs.append(num)
            tops.append(top)
            sums.append(den)
        build(last_send, jj, outs, tops, sums)

        @pl.when(k < nbr)
        def _():
            f_copy(jj, my_br).start()

        return c

    lax.fori_loop(1, nbr + 1, gather, 0)
    last_recv[my_br] = last_send[my_br]

    def merge(k, c):
        jj = along(k)

        @pl.when(k > 0)
        def _():
            f_copy(my_br, jj).wait_recv()

        row_top, row_sum = read_stats(last_recv, jj)
        finals = []
        for h in range(kvl):
            height = to_column(h, row_top)
            mine = own_w[jj, h]
            top = jnp.maximum(mine, height)
            first_scale = jnp.exp2((mine - top) * factor)
            scale = jnp.exp2((height - top) * factor)
            piece = last_recv[jj, h * mrow : (h + 1) * mrow, :].astype(F32)
            num = own_v[jj, h] * first_scale + piece * scale
            den = first_scale + to_column(h, row_sum) * scale
            finals.append((num / den).reshape(rdev, group, hd))
        out_ref[:, jj] = jnp.concatenate(finals, axis=1).astype(BF16)
        return c

    lax.fori_loop(0, nbr, merge, 0)

    def drain_branch(k, c):
        q_copy(along(k), my_br).wait_send()
        f_copy(along(k), my_br).wait_send()
        return c

    lax.fori_loop(1, nbr, drain_branch, 0)

    def drain_blk(d, c):
        ib = near(d)

        def drain_pass(j, c):
            pass_copy(ib, j, my_blk).wait_send()
            return c

        p_copy(ib, my_blk).wait_send()
        return lax.fori_loop(0, nbr, drain_pass, c)

    lax.fori_loop(1, nblk, drain_blk, 0)


def solution(mesh):
    nblk, nbr = mesh.shape["blk"], mesh.shape["branch"]

    def per_device(q, nk, nv, pk, pv, sk, sv, lens, slots):
        rdev, heads, hd = q.shape
        keys, kvl = pk.shape[:2]
        nslot, suf = sk.shape[:2]
        hl = heads // nbr
        group = hl // kvl
        n = nblk * nbr
        rows = rdev * nbr
        mrow = rdev * group
        cfg = (nblk, nbr, rdev, kvl, group, hd, keys, suf)
        dma = pltpu.SemaphoreType.DMA
        out = pl.pallas_call(
            functools.partial(kernel, cfg),
            out_shape=jax.ShapeDtypeStruct((rdev, nbr, hl, hd), BF16),
            in_specs=[pl.BlockSpec(memory_space=pl.ANY)] * 9,
            out_specs=pl.BlockSpec(memory_space=pltpu.VMEM),
            scratch_shapes=[
                pltpu.VMEM((rdev, nbr, hl, hd), BF16),
                pltpu.VMEM(nk.shape, BF16),
                pltpu.VMEM(nv.shape, BF16),
                pltpu.VMEM((keys * kvl, hd), BF16),
                pltpu.VMEM((keys * kvl, hd), BF16),
                pltpu.VMEM((keys * kvl, hd), F32),
                pltpu.VMEM((keys * kvl, hd), F32),
                pltpu.VMEM((kvl, keys, hd), BF16),
                pltpu.VMEM((kvl, keys, hd), BF16),
                pltpu.VMEM((nslot, suf * kvl, hd), BF16),
                pltpu.VMEM((nslot, suf * kvl, hd), BF16),
                pltpu.SMEM(lens.shape, jnp.int32),
                pltpu.SMEM(slots.shape, jnp.int32),
                pltpu.VMEM((n * rdev, hl, hd), BF16),
                pltpu.VMEM((kvl, rows * group, hd), F32),
                pltpu.VMEM((kvl, rows * group, hd), F32),
                pltpu.VMEM((kvl, rows * group, hd), F32),
                pltpu.VMEM((kvl, rows * group, hd), F32),
                pltpu.VMEM((kvl, rows * group, hd), F32),
                pltpu.VMEM((kvl, rows * group, hd), F32),
                pltpu.VMEM((nbr, kvl, mrow, hd), F32),
                pltpu.VMEM((nbr, kvl, mrow, hd), F32),
                pltpu.VMEM((n, kvl * mrow + STAT_ROWS, hd), BF16),
                pltpu.VMEM((n, kvl * mrow + STAT_ROWS, hd), BF16),
                pltpu.VMEM((nbr, kvl * mrow + STAT_ROWS, hd), BF16),
                pltpu.VMEM((nbr, kvl * mrow + STAT_ROWS, hd), BF16),
                dma((10,)),
                dma((nbr,)),
                dma((nbr,)),
                dma((n,)),
                dma((n,)),
                dma((nblk,)),
                dma((nblk,)),
                dma((nbr,)),
                dma((nbr,)),
            ],
            compiler_params=pltpu.CompilerParams(
                collective_id=0, has_side_effects=True, vmem_limit_bytes=60 * 1024 * 1024
            ),
            name="attend",
        )(
            q.reshape(rdev, nbr, hl, hd),
            nk,
            nv,
            pk.reshape(keys * kvl, hd),
            pv.reshape(keys * kvl, hd),
            sk.reshape(nslot, suf * kvl, hd),
            sv.reshape(nslot, suf * kvl, hd),
            lens,
            slots,
        )
        return out.reshape(rdev, heads, hd)

    return jax.shard_map(
        per_device,
        mesh=mesh,
        in_specs=(
            P(("groups", "blk", "branch"), None, None),
            P(("groups", "blk", "branch"), None, None),
            P(("groups", "blk", "branch"), None, None),
            P(("groups", "blk"), "branch", None),
            P(("groups", "blk"), "branch", None),
            P(("groups", "blk"), None, "branch", None),
            P(("groups", "blk"), None, "branch", None),
            P("groups"),
            P("groups"),
        ),
        out_specs=P(("groups", "blk", "branch"), None, None),
        check_vma=False,
    )
```
